32 devices in a mesh: groups: 2 (over x), track: 8 (over z, y), sub: 2 (over core).
Axes of the slice: x: 2, y: 2, z: 4, core: 2. Of those that a mesh axis runs over, the one named last changes fastest.
Arguments:
- tokens: bfloat16 [512, 128, 384], P(('groups', 'track', 'sub')), parts along dimension 0, may hold values from -6 to 6
- visible: int32 [512, 2], P(('groups', 'track', 'sub')), parts along dimension 0, may hold values from 0 to 128, as said below
- time_attn: bfloat16 [4, 384, 384], replicated, may hold values from -0.3125 to 0.3125
- mlp_in: bfloat16 [384, 1536], replicated, may hold values from -0.3125 to 0.3125
- mlp_out: bfloat16 [1536, 384], replicated, may hold values from -0.15625 to 0.15625
- virt_attn: bfloat16 [3, 4, 384, 384], replicated, may hold values from -0.3125 to 0.3125
- virtual: bfloat16 [64, 384], replicated, may hold values from -6 to 6
Outputs:
- updated: bfloat16 [512, 128, 384], P(('groups', 'track', 'sub')), parts along dimension 0
The draws below stay inside these ranges and needn't reach their ends.
There are 2 independent parts, one for each index of `groups`. The reference program is written for one: setup_inputs(seed, part) draws one part's arguments, and reference() takes and returns one part's arrays. A program takes and returns all parts, laid end to end along the dimension named above; an argument that names none is the same for every part. Nothing has to cross between parts.
Inputs may be any that keep to these rules, and one draw needn't show every extreme that they name: visible[n, 0] < visible[n, 1]; the first track of every block of 16 tracks is visible in all 128 frames.
All inputs are finite; a program needn't handle non-finite values.
Results may differ from the reference program's by a relative error of at most 0.0095.
Values may be sent and summed in bfloat16 or wider, within the bound.
A program may use at most 128 MiB of HBM per device.

```python
import math
import jax
import jax.numpy as jnp
from jax import lax

D = 384
FF = 1536
HEADS = 8
VIRT = 64
TRK_DEV = 16
TRACKS = 256
FRAMES = 128


def draw_visible(key, part):
    key_limit, key_length, key_offset = jax.random.split(key, 3)
    blocks = TRACKS // TRK_DEV
    limits = jax.random.randint(key_limit, (blocks, 1), max(FRAMES // 4, 1), FRAMES + 1)
    lengths = jax.random.randint(key_length, (blocks, TRK_DEV), 0, 1048576) % limits + 1
    column = jnp.arange(TRK_DEV, dtype=jnp.int32)[None, :]
    lengths = jnp.where(column == 0, FRAMES, lengths).reshape(TRACKS)
    offsets = jax.random.randint(key_offset, (TRACKS,), 0, 1048576) % (FRAMES - lengths + 1)
    return jnp.stack([offsets, offsets + lengths], axis=1).astype(jnp.int32)


def shard_levels(key, dims, shards, smallest, top_value):
    gain, own = 1.0, jax.random.fold_in(key, 6)
    for axis_at, shards_of in shards:
        heights = jnp.exp(jax.random.uniform(jax.random.fold_in(own, axis_at), (shards_of,), jnp.float32, smallest / len(shards), top_value / len(shards)))
        gain = gain * jnp.repeat(heights, dims[axis_at] // shards_of).reshape([-1 if axis == axis_at else 1 for axis in range(len(dims))])
    return gain


def gaussian(stream_key, dims, deviation, limit, cuts=(), kind=jnp.bfloat16):
    values = deviation * jax.random.normal(stream_key, dims, jnp.float32)
    if cuts:
        values = values * shard_levels(stream_key, dims, cuts, -0.22, 0.18)
    return jnp.clip(values, -limit, limit).astype(kind)


def setup_inputs(seed: int = 0, part: int = 0) -> dict:
    splits = jax.random.split(jax.random.key(seed), 8)
    part_keys = jax.random.split(jax.random.fold_in(splits[7], part), 8)
    tokens = gaussian(part_keys[0], (TRACKS, FRAMES, D), 1.0, 6.0, ((0, 16),))
    visible = draw_visible(jax.random.fold_in(jax.random.fold_in(splits[7], part), 71), part)
    time_attn = gaussian(splits[2], (4, D, D), D ** -0.5, 0.3125)
    mlp_in = gaussian(splits[3], (D, FF), D ** -0.5, 0.3125)
    mlp_out = gaussian(splits[4], (FF, D), FF ** -0.5, 0.15625)
    virt_attn = gaussian(splits[5], (3, 4, D, D), D ** -0.5, 0.3125)
    virtual = gaussian(splits[6], (VIRT, D), 1.0, 6.0)
    return dict(tokens=tokens, visible=visible, time_attn=time_attn, mlp_in=mlp_in, mlp_out=mlp_out, virt_attn=virt_attn, virtual=virtual)


def layer_norm(values):
    wide = values.astype(jnp.float32)
    center = wide - lax.optimization_barrier(jnp.mean(wide, axis=-1, keepdims=True))
    spread = lax.optimization_barrier(jnp.mean(center * center, axis=-1, keepdims=True))
    return (center * lax.rsqrt(spread + 1e-05)).astype(jnp.bfloat16)

def project(values, matrix):
    return jnp.dot(values, matrix, preferred_element_type=jnp.float32)

def attend(queries, key_rows, value_rows, mask):
    n_batch, n_query, feature = queries.shape
    n_keys = key_rows.shape[1]
    head_size = feature // HEADS
    query_h = queries.reshape(n_batch, n_query, HEADS, head_size).astype(jnp.float32)
    key_h = key_rows.reshape(n_batch, n_keys, HEADS, head_size).astype(jnp.float32)
    value_h = value_rows.reshape(n_batch, n_keys, HEADS, head_size).astype(jnp.float32)
    scores = jnp.einsum('bqhe,bkhe->bhqk', query_h, key_h) * (1.0 / math.sqrt(head_size))
    if mask is not None:
        scores = jnp.where(mask, scores, -1e+30)
    weights = jax.nn.softmax(scores, axis=-1).astype(jnp.bfloat16)
    mixed = jnp.einsum('bhqk,bkhe->bqhe', weights.astype(jnp.float32), value_h).astype(jnp.bfloat16)
    return mixed.reshape(n_batch, n_query, feature)

def time_block(tokens, visible, time_attn, mlp_in, mlp_out):
    frame_ids = jnp.arange(tokens.shape[1], dtype=jnp.int32)
    seen = (frame_ids[None, :] >= visible[:, 0:1]) & (frame_ids[None, :] < visible[:, 1:2])
    vis = seen.astype(jnp.float32)[:, :, None]
    normed = layer_norm(tokens)
    queries = project(normed, time_attn[0]).astype(jnp.bfloat16)
    key_rows = project(normed, time_attn[1]).astype(jnp.bfloat16)
    value_rows = project(normed, time_attn[2]).astype(jnp.bfloat16)
    mixed = attend(queries, key_rows, value_rows, seen[:, None, None, :])
    first = tokens.astype(jnp.float32) + vis * project(mixed, time_attn[3])
    hidden = jax.nn.gelu(project(layer_norm(first), mlp_in), approximate=True).astype(jnp.bfloat16)
    return (first + vis * project(hidden, mlp_out)).astype(jnp.bfloat16)

def frame_block(framed, virt_attn, virtual):
    n_frames = framed.shape[0]
    normed = layer_norm(framed)
    key_c = project(normed, virt_attn[0, 1]).astype(jnp.bfloat16)
    value_c = project(normed, virt_attn[0, 2]).astype(jnp.bfloat16)
    query_c = project(layer_norm(virtual), virt_attn[0, 0]).astype(jnp.bfloat16)
    query_c = jnp.broadcast_to(query_c[None], (n_frames,) + query_c.shape)
    cross = attend(query_c, key_c, value_c, None)
    first = virtual.astype(jnp.float32)[None] + project(cross, virt_attn[0, 3])
    normed_w = layer_norm(first)
    query_s = project(normed_w, virt_attn[1, 0]).astype(jnp.bfloat16)
    key_s = project(normed_w, virt_attn[1, 1]).astype(jnp.bfloat16)
    value_s = project(normed_w, virt_attn[1, 2]).astype(jnp.bfloat16)
    second = first + project(attend(query_s, key_s, value_s, None), virt_attn[1, 3])
    normed_b = layer_norm(second)
    key_b = project(normed_b, virt_attn[2, 1]).astype(jnp.bfloat16)
    value_b = project(normed_b, virt_attn[2, 2]).astype(jnp.bfloat16)
    query_b = project(normed, virt_attn[2, 0]).astype(jnp.bfloat16)
    back = attend(query_b, key_b, value_b, None)
    return (framed.astype(jnp.float32) + project(back, virt_attn[2, 3])).astype(jnp.bfloat16)

def reference(tokens, visible, time_attn, mlp_in, mlp_out, virt_attn, virtual):
    block = 16
    grouped = tokens.reshape(TRACKS // block, block, FRAMES, D)
    grouped_vis = visible.reshape(TRACKS // block, block, 2)
    after = lax.map(lambda pair: time_block(pair[0], pair[1], time_attn, mlp_in, mlp_out), (grouped, grouped_vis))
    after = after.reshape(TRACKS, FRAMES, D)
    framed = jnp.swapaxes(after, 0, 1).reshape(FRAMES, 1, TRACKS, D)
    result = lax.map(lambda single: frame_block(single, virt_attn, virtual), framed)
    return jnp.swapaxes(result.reshape(FRAMES, TRACKS, D), 0, 1)
```

```python
import functools
import math

import jax
import jax.numpy as jnp
from jax import lax
from jax.experimental import pallas as pl
from jax.experimental.pallas import tpu as pltpu
from jax.sharding import PartitionSpec as P

HEADS = 8
F32 = jnp.float32
BF16 = jnp.bfloat16


def layer_norm(values):
    wide = values.astype(F32)
    center = wide - jnp.mean(wide, axis=-1, keepdims=True)
    spread = jnp.mean(center * center, axis=-1, keepdims=True)
    return (center * lax.rsqrt(spread + 1e-05)).astype(BF16)


def project(values, matrix):
    return jnp.dot(values, matrix, preferred_element_type=F32)


def product(left, right, left_dim, right_dim):
    dims = (((left_dim,), (right_dim,)), ((), ()))
    return lax.dot_general(left, right, dims, preferred_element_type=F32)


def head_masks(feature, kind):
    size = feature // HEADS
    lanes = lax.broadcasted_iota(jnp.int32, (1, feature), 1)
    return [
        jnp.where((lanes >= head * size) & (lanes < (head + 1) * size), 1.0, 0.0).astype(kind)
        for head in range(HEADS)
    ]


def spread_heads(rows, masks):
    return jnp.concatenate([rows * mask for mask in masks], axis=0)


def time_step(tokens, first_frame, end_frame, attn_ref, in_ref, out_ref, ones_ref):
    tracks, frames, feature = tokens.shape
    scale = 1.0 / math.sqrt(feature // HEADS)
    masks = head_masks(feature, BF16)
    wide = tokens.reshape(tracks * frames, feature).astype(F32)
    normed = layer_norm(wide)
    queries = project(normed, attn_ref[0]).astype(BF16)
    keys = project(normed, attn_ref[1]).astype(BF16)
    values = project(normed, attn_ref[2]).astype(BF16)
    lane = lax.broadcasted_iota(jnp.int32, (1, frames), 1)
    row = lax.broadcasted_iota(jnp.int32, (frames, feature), 0)
    mixed, vis = [], []
    for track in range(tracks):
        part = slice(track * frames, (track + 1) * frames)
        seen = (lane >= first_frame[track]) & (lane < end_frame[track])
        scores = product(queries[part], spread_heads(keys[part], masks), 1, 1)
        weights = []
        for head in range(HEADS):
            own = scores[:, head * frames : (head + 1) * frames] * scale
            own = jnp.where(seen, own, -1e30)
            top = jnp.max(own, axis=-1, keepdims=True)
            weights.append(jnp.exp(own - top).astype(BF16))
        weights = jnp.concatenate(weights, axis=1)
        summed = project(weights, spread_heads(values[part], masks))
        total = project(weights, ones_ref[...])
        mixed.append((summed / total).astype(BF16))
        shown = (row >= first_frame[track]) & (row < end_frame[track])
        vis.append(jnp.where(shown, 1.0, 0.0).astype(F32))
    mixed = jnp.concatenate(mixed, axis=0)
    vis = jnp.concatenate(vis, axis=0)
    first = wide + vis * project(mixed, attn_ref[3])
    hidden = jax.nn.gelu(project(layer_norm(first), in_ref[...]), approximate=True).astype(BF16)
    return first + vis * project(hidden, out_ref[...])


def fill_ones(ones_ref, feature):
    rows = ones_ref.shape[0] // HEADS
    for head, mask in enumerate(head_masks(feature, F32)):
        ones_ref[head * rows : (head + 1) * rows, :] = jnp.broadcast_to(mask, (rows, feature)).astype(BF16)


def few_queries(spread_queries, keys, values, masks):
    feature = keys.shape[1]
    scores = product(spread_queries, keys, 1, 1) * (1.0 / math.sqrt(feature // HEADS))
    top = jnp.max(scores, axis=-1, keepdims=True)
    weights = jnp.exp(scores - top)
    total = jnp.sum(weights, axis=-1, keepdims=True)
    summed = project(weights.astype(BF16), values) / total
    count = spread_queries.shape[0] // HEADS
    mixed = summed[:count] * masks[0]
    for head in range(1, HEADS):
        mixed = mixed + summed[head * count : (head + 1) * count] * masks[head]
    return mixed.astype(BF16)


def frame_step(framed, attn_ref, virtual_ref, query_ref, ones_ref):
    frames, tracks, feature = framed.shape
    n_virtual = virtual_ref.shape[0]
    scale = 1.0 / math.sqrt(feature // HEADS)
    masks = head_masks(feature, BF16)
    wide_masks = head_masks(feature, F32)
    wide = framed.reshape(frames * tracks, feature).astype(F32)
    normed = layer_norm(wide)
    key_c = project(normed, attn_ref[0, 1]).astype(BF16)
    value_c = project(normed, attn_ref[0, 2]).astype(BF16)
    query_b = project(normed, attn_ref[2, 0]).astype(BF16)
    track_part = [slice(f * tracks, (f + 1) * tracks) for f in range(frames)]
    virtual_part = [slice(f * n_virtual, (f + 1) * n_virtual) for f in range(frames)]
    cross = [few_queries(query_ref[...], key_c[part], value_c[part], wide_masks) for part in track_part]
    base = jnp.concatenate([virtual_ref[...].astype(F32)] * frames, axis=0)
    first = base + project(jnp.concatenate(cross, axis=0), attn_ref[0, 3])
    normed_w = layer_norm(first)
    query_s = project(normed_w, attn_ref[1, 0]).astype(BF16)
    key_s = project(normed_w, attn_ref[1, 1]).astype(BF16)
    value_s = project(normed_w, attn_ref[1, 2]).astype(BF16)
    among = [
        few_queries(spread_heads(query_s[part], masks), key_s[part], value_s[part], wide_masks)
        for part in virtual_part
    ]
    second = first + project(jnp.concatenate(among, axis=0), attn_ref[1, 3])
    normed_b = layer_norm(second)
    key_b = project(normed_b, attn_ref[2, 1]).astype(BF16)
    value_b = project(normed_b, attn_ref[2, 2]).astype(BF16)
    back = []
    for frame in range(frames):
        part = virtual_part[frame]
        scores = product(spread_heads(key_b[part], masks), query_b[track_part[frame]], 1, 1) * scale
        scores = scores.reshape(HEADS, n_virtual, tracks)
        top = jnp.max(scores, axis=1, keepdims=True)
        weights = jnp.exp(scores - top).astype(BF16).reshape(HEADS * n_virtual, tracks)
        summed = product(weights, spread_heads(value_b[part], masks), 0, 0)
        total = product(weights, ones_ref[...], 0, 0)
        back.append((summed / total).astype(BF16))
    return wide + project(jnp.concatenate(back, axis=0), attn_ref[2, 3])


def time_kernel(vis_ref, tok_ref, attn_ref, in_ref, out_ref, x_ref, ones_ref):
    step = pl.program_id(0)
    tracks, frames, feature = tok_ref.shape

    @pl.when(step == 0)
    def _():
        fill_ones(ones_ref, feature)

    begin = [vis_ref[step * tracks + i, 0] for i in range(tracks)]
    end = [vis_ref[step * tracks + i, 1] for i in range(tracks)]
    after = time_step(tok_ref[...], begin, end, attn_ref, in_ref, out_ref, ones_ref)
    x_ref[...] = after.astype(BF16).reshape(tracks, frames, feature)


def frame_kernel(x_ref, attn_ref, virtual_ref, y_ref, query_ref, ones_ref):
    frames, tracks, feature = x_ref.shape

    @pl.when(pl.program_id(0) == 0)
    def _():
        fill_ones(ones_ref, feature)
        query = project(layer_norm(virtual_ref[...]), attn_ref[0, 0]).astype(BF16)
        query_ref[...] = spread_heads(query, head_masks(feature, BF16))

    after = frame_step(x_ref[...], attn_ref, virtual_ref, query_ref, ones_ref)
    y_ref[...] = after.astype(BF16).reshape(frames, tracks, feature)


WHOLE = pl.BlockSpec(memory_space=pltpu.VMEM)
LIMIT = 60 * 1024 * 1024


def time_block(tokens, visible, time_attn, mlp_in, mlp_out, group):
    tracks, frames, feature = tokens.shape
    spec = pl.BlockSpec((group, frames, feature), lambda i: (i, 0, 0))
    return pl.pallas_call(
        time_kernel,
        grid=(tracks // group,),
        in_specs=[pl.BlockSpec(memory_space=pltpu.SMEM), spec, WHOLE, WHOLE, WHOLE],
        out_specs=spec,
        out_shape=jax.ShapeDtypeStruct(tokens.shape, BF16),
        scratch_shapes=[pltpu.VMEM((HEADS * frames, feature), BF16)],
        compiler_params=pltpu.CompilerParams(vmem_limit_bytes=LIMIT),
    )(visible, tokens, time_attn, mlp_in, mlp_out)


def frame_block(framed, virt_attn, virtual, group):
    frames, tracks, feature = framed.shape
    n_virtual = virtual.shape[0]
    spec = pl.BlockSpec((group, tracks, feature), lambda i: (i, 0, 0))
    return pl.pallas_call(
        frame_kernel,
        grid=(frames // group,),
        in_specs=[spec, WHOLE, WHOLE],
        out_specs=spec,
        out_shape=jax.ShapeDtypeStruct(framed.shape, BF16),
        scratch_shapes=[
            pltpu.VMEM((HEADS * n_virtual, feature), BF16),
            pltpu.VMEM((HEADS * n_virtual, feature), BF16),
        ],
        compiler_params=pltpu.CompilerParams(vmem_limit_bytes=LIMIT),
    )(framed, virt_attn, virtual)


def shards(tokens, visible, time_attn, mlp_in, mlp_out, virt_attn, virtual):
    after = time_block(tokens, visible, time_attn, mlp_in, mlp_out, 2)
    by_frame = lax.all_to_all(after, ("track", "sub"), split_axis=1, concat_axis=0, tiled=True)
    framed = jnp.swapaxes(by_frame, 0, 1)
    mixed = jnp.swapaxes(frame_block(framed, virt_attn, virtual, 2), 0, 1)
    return lax.all_to_all(mixed, ("track", "sub"), split_axis=0, concat_axis=1, tiled=True)


def solution(mesh):
    placed = (
        P(("groups", "track", "sub"), None, None),
        P(("groups", "track", "sub"), None),
        P(),
        P(),
        P(),
        P(),
        P(),
    )
    return jax.shard_map(
        shards,
        mesh=mesh,
        in_specs=placed,
        out_specs=P(("groups", "track", "sub"), None, None),
        check_vma=False,
    )
```

```python
import functools
import math

import jax
import jax.numpy as jnp
from jax import lax
from jax.experimental import pallas as pl
from jax.experimental.pallas import tpu as pltpu
from jax.sharding import PartitionSpec as P

HEADS = 8
F32 = jnp.float32
BF16 = jnp.bfloat16


def layer_norm(values):
    wide = values.astype(F32)
    center = wide - jnp.mean(wide, axis=-1, keepdims=True)
    spread = jnp.mean(center * center, axis=-1, keepdims=True)
    return (center * lax.rsqrt(spread + 1e-05)).astype(BF16)


def project(values, matrix):
    return jnp.dot(values, matrix, preferred_element_type=F32)


def product(left, right, left_dim, right_dim):
    dims = (((left_dim,), (right_dim,)), ((), ()))
    return lax.dot_general(left, right, dims, preferred_element_type=F32)


def head_masks(feature, kind):
    size = feature // HEADS
    lanes = lax.broadcasted_iota(jnp.int32, (1, feature), 1)
    return [
        jnp.where((lanes >= head * size) & (lanes < (head + 1) * size), 1.0, 0.0).astype(kind)
        for head in range(HEADS)
    ]


def spread_heads(rows, masks):
    return jnp.concatenate([rows * mask for mask in masks], axis=0)


def time_step(tokens, first_frame, end_frame, attn_ref, in_ref, out_ref, ones_ref):
    tracks, frames, feature = tokens.shape
    scale = 1.0 / math.sqrt(feature // HEADS)
    masks = head_masks(feature, BF16)
    wide = tokens.reshape(tracks * frames, feature).astype(F32)
    normed = layer_norm(wide)
    queries = project(normed, attn_ref[0]).astype(BF16)
    keys = project(normed, attn_ref[1]).astype(BF16)
    values = project(normed, attn_ref[2]).astype(BF16)
    lane = lax.broadcasted_iota(jnp.int32, (1, frames), 1)
    row = lax.broadcasted_iota(jnp.int32, (frames, feature), 0)
    mixed, vis = [], []
    for track in range(tracks):
        part = slice(track * frames, (track + 1) * frames)
        seen = (lane >= first_frame[track]) & (lane < end_frame[track])
        scores = product(queries[part], spread_heads(keys[part], masks), 1, 1)
        weights = []
        for head in range(HEADS):
            own = scores[:, head * frames : (head + 1) * frames] * scale
            own = jnp.where(seen, own, -1e30)
            top = jnp.max(own, axis=-1, keepdims=True)
            weights.append(jnp.exp(own - top).astype(BF16))
        weights = jnp.concatenate(weights, axis=1)
        summed = project(weights, spread_heads(values[part], masks))
        total = project(weights, ones_ref[...])
        mixed.append((summed / total).astype(BF16))
        shown = (row >= first_frame[track]) & (row < end_frame[track])
        vis.append(jnp.where(shown, 1.0, 0.0).astype(F32))
    mixed = jnp.concatenate(mixed, axis=0)
    vis = jnp.concatenate(vis, axis=0)
    first = wide + vis * project(mixed, attn_ref[3])
    hidden = jax.nn.gelu(project(layer_norm(first), in_ref[...]), approximate=True).astype(BF16)
    return first + vis * project(hidden, out_ref[...])


def fill_ones(ones_ref, feature):
    rows = ones_ref.shape[0] // HEADS
    for head, mask in enumerate(head_masks(feature, F32)):
        ones_ref[head * rows : (head + 1) * rows, :] = jnp.broadcast_to(mask, (rows, feature)).astype(BF16)


def few_queries(spread_queries, keys, values, masks):
    feature = keys.shape[1]
    scores = product(spread_queries, keys, 1, 1) * (1.0 / math.sqrt(feature // HEADS))
    top = jnp.max(scores, axis=-1, keepdims=True)
    weights = jnp.exp(scores - top)
    total = jnp.sum(weights, axis=-1, keepdims=True)
    summed = project(weights.astype(BF16), values) / total
    count = spread_queries.shape[0] // HEADS
    mixed = summed[:count] * masks[0]
    for head in range(1, HEADS):
        mixed = mixed + summed[head * count : (head + 1) * count] * masks[head]
    return mixed.astype(BF16)


def frame_step(framed, attn_ref, virtual_ref, query_ref, ones_ref):
    frames, tracks, feature = framed.shape
    n_virtual = virtual_ref.shape[0]
    scale = 1.0 / math.sqrt(feature // HEADS)
    masks = head_masks(feature, BF16)
    wide_masks = head_masks(feature, F32)
    wide = framed.reshape(frames * tracks, feature).astype(F32)
    normed = layer_norm(wide)
    key_c = project(normed, attn_ref[0, 1]).astype(BF16)
    value_c = project(normed, attn_ref[0, 2]).astype(BF16)
    query_b = project(normed, attn_ref[2, 0]).astype(BF16)
    track_part = [slice(f * tracks, (f + 1) * tracks) for f in range(frames)]
    virtual_part = [slice(f * n_virtual, (f + 1) * n_virtual) for f in range(frames)]
    cross = [few_queries(query_ref[...], key_c[part], value_c[part], wide_masks) for part in track_part]
    base = jnp.concatenate([virtual_ref[...].astype(F32)] * frames, axis=0)
    first = base + project(jnp.concatenate(cross, axis=0), attn_ref[0, 3])
    normed_w = layer_norm(first)
    query_s = project(normed_w, attn_ref[1, 0]).astype(BF16)
    key_s = project(normed_w, attn_ref[1, 1]).astype(BF16)
    value_s = project(normed_w, attn_ref[1, 2]).astype(BF16)
    among = [
        few_queries(spread_heads(query_s[part], masks), key_s[part], value_s[part], wide_masks)
        for part in virtual_part
    ]
    second = first + project(jnp.concatenate(among, axis=0), attn_ref[1, 3])
    normed_b = layer_norm(second)
    key_b = project(normed_b, attn_ref[2, 1]).astype(BF16)
    value_b = project(normed_b, attn_ref[2, 2]).astype(BF16)
    back = []
    for frame in range(frames):
        part = virtual_part[frame]
        scores = product(spread_heads(key_b[part], masks), query_b[track_part[frame]], 1, 1) * scale
        scores = scores.reshape(HEADS, n_virtual, tracks)
        top = jnp.max(scores, axis=1, keepdims=True)
        weights = jnp.exp(scores - top).astype(BF16).reshape(HEADS * n_virtual, tracks)
        summed = product(weights, spread_heads(value_b[part], masks), 0, 0)
        total = product(weights, ones_ref[...], 0, 0)
        back.append((summed / total).astype(BF16))
    return wide + project(jnp.concatenate(back, axis=0), attn_ref[2, 3])


class Exchange:
    def __init__(self, shape, slab_ref, dest_ref, send_sem, recv_sem, local_sem):
        self.n_sub = shape["sub"]
        self.count = shape["track"] * shape["sub"]
        self.me = lax.axis_index("track") * self.n_sub + lax.axis_index("sub")
        self.slab_ref, self.dest_ref = slab_ref, dest_ref
        self.send_sem, self.recv_sem, self.local_sem = send_sem, recv_sem, local_sem
        self.offsets = sorted(range(1, self.count), key=lambda j: abs(2 * j - self.count))

    def device(self, peer):
        return {"track": peer // self.n_sub, "sub": peer % self.n_sub}

    def greet(self):
        barrier = pltpu.get_barrier_semaphore()
        for offset in self.offsets:
            pl.semaphore_signal(
                barrier,
                inc=1,
                device_id=self.device(lax.rem(self.me + offset, self.count)),
                device_id_type=pl.DeviceIdType.MESH,
            )

    def admit(self):
        pl.semaphore_wait(pltpu.get_barrier_semaphore(), self.count - 1)

    def send(self, begin, rows):
        each = self.slab_ref.shape[1]
        target = self.dest_ref.at[pl.ds(self.me * each + begin, rows)]
        for offset in self.offsets:
            peer = lax.rem(self.me + offset, self.count)
            pltpu.make_async_remote_copy(
                src_ref=self.slab_ref.at[peer, pl.ds(begin, rows)],
                dst_ref=target,
                send_sem=self.send_sem,
                recv_sem=self.recv_sem,
                device_id=self.device(peer),
                device_id_type=pl.DeviceIdType.MESH,
            ).start()
        pltpu.make_async_copy(self.slab_ref.at[self.me, pl.ds(begin, rows)], target, self.local_sem).start()

    def finish(self):
        each = self.slab_ref.shape[1]
        others = self.dest_ref.at[pl.ds(0, (self.count - 1) * each)]
        own = self.dest_ref.at[pl.ds(self.me * each, each)]
        pltpu.make_async_copy(own, own, self.local_sem).wait()
        pltpu.make_async_copy(others, others, self.send_sem).wait()
        pltpu.make_async_copy(others, others, self.recv_sem).wait()


def time_kernel(shape, vis_ref, tok_ref, attn_ref, in_ref, out_ref, dest_ref, ones_ref, slab_ref, *sems):
    step = pl.program_id(0)
    tracks, frames, feature = tok_ref.shape
    exchange = Exchange(shape, slab_ref, dest_ref, *sems)

    @pl.when(step == 0)
    def _():
        exchange.greet()
        fill_ones(ones_ref, feature)

    begin = [vis_ref[step * tracks + i, 0] for i in range(tracks)]
    end = [vis_ref[step * tracks + i, 1] for i in range(tracks)]
    after = time_step(tok_ref[...], begin, end, attn_ref, in_ref, out_ref, ones_ref)
    for i in range(tracks):
        block = after[i * frames : (i + 1) * frames].reshape(exchange.count, frames // exchange.count, feature)
        slab_ref[:, step * tracks + i] = block.astype(BF16)

    @pl.when(step == 0)
    def _():
        exchange.admit()

    exchange.send(step * tracks, tracks)

    @pl.when(step == pl.num_programs(0) - 1)
    def _():
        exchange.finish()


def frame_kernel(shape, x_ref, attn_ref, virtual_ref, dest_ref, query_ref, ones_ref, slab_ref, *sems):
    step = pl.program_id(0)
    frames, tracks, feature = x_ref.shape
    exchange = Exchange(shape, slab_ref, dest_ref, *sems)

    @pl.when(step == 0)
    def _():
        exchange.greet()
        fill_ones(ones_ref, feature)
        query = project(layer_norm(virtual_ref[...]), attn_ref[0, 0]).astype(BF16)
        query_ref[...] = spread_heads(query, head_masks(feature, BF16))

    after = frame_step(x_ref[...], attn_ref, virtual_ref, query_ref, ones_ref).astype(BF16)
    for f in range(frames):
        block = after[f * tracks : (f + 1) * tracks].reshape(exchange.count, tracks // exchange.count, feature)
        slab_ref[:, step * frames + f] = block

    @pl.when(step == 0)
    def _():
        exchange.admit()

    exchange.send(step * frames, frames)

    @pl.when(step == pl.num_programs(0) - 1)
    def _():
        exchange.finish()


WHOLE = pl.BlockSpec(memory_space=pltpu.VMEM)
LIMIT = 60 * 1024 * 1024
SEMS = [pltpu.SemaphoreType.DMA, pltpu.SemaphoreType.DMA, pltpu.SemaphoreType.DMA]


def time_block(shape, tokens, visible, time_attn, mlp_in, mlp_out, group):
    tracks, frames, feature = tokens.shape
    count = shape["track"] * shape["sub"]
    each = frames // count
    spec = pl.BlockSpec((group, frames, feature), lambda i: (i, 0, 0))
    return pl.pallas_call(
        functools.partial(time_kernel, shape),
        grid=(tracks // group,),
        in_specs=[pl.BlockSpec(memory_space=pltpu.SMEM), spec, WHOLE, WHOLE, WHOLE],
        out_specs=pl.BlockSpec(memory_space=pl.ANY),
        out_shape=jax.ShapeDtypeStruct((count * tracks, each, feature), BF16),
        scratch_shapes=[
            pltpu.VMEM((HEADS * frames, feature), BF16),
            pltpu.VMEM((count, tracks, each, feature), BF16),
        ]
        + SEMS,
        compiler_params=pltpu.CompilerParams(vmem_limit_bytes=LIMIT, collective_id=0, has_side_effects=True),
    )(visible, tokens, time_attn, mlp_in, mlp_out)


def frame_block(shape, framed, virt_attn, virtual, group):
    frames, tracks, feature = framed.shape
    n_virtual = virtual.shape[0]
    count = shape["track"] * shape["sub"]
    each = tracks // count
    spec = pl.BlockSpec((group, tracks, feature), lambda i: (i, 0, 0))
    return pl.pallas_call(
        functools.partial(frame_kernel, shape),
        grid=(frames // group,),
        in_specs=[spec, WHOLE, WHOLE],
        out_specs=pl.BlockSpec(memory_space=pl.ANY),
        out_shape=jax.ShapeDtypeStruct((count * frames, each, feature), BF16),
        scratch_shapes=[
            pltpu.VMEM((HEADS * n_virtual, feature), BF16),
            pltpu.VMEM((HEADS * n_virtual, feature), BF16),
            pltpu.VMEM((count, frames, each, feature), BF16),
        ]
        + SEMS,
        compiler_params=pltpu.CompilerParams(vmem_limit_bytes=LIMIT, collective_id=1, has_side_effects=True),
    )(framed, virt_attn, virtual)


def shards(shape, tokens, visible, time_attn, mlp_in, mlp_out, virt_attn, virtual):
    by_frame = time_block(shape, tokens, visible, time_attn, mlp_in, mlp_out, 2)
    framed = jnp.swapaxes(by_frame, 0, 1)
    return jnp.swapaxes(frame_block(shape, framed, virt_attn, virtual, 2), 0, 1)


def solution(mesh):
    placed = (
        P(("groups", "track", "sub"), None, None),
        P(("groups", "track", "sub"), None),
        P(),
        P(),
        P(),
        P(),
        P(),
    )
    return jax.shard_map(
        functools.partial(shards, dict(mesh.shape)),
        mesh=mesh,
        in_specs=placed,
        out_specs=P(("groups", "track", "sub"), None, None),
        check_vma=False,
    )
```

```python
import functools
import math

import jax
import jax.numpy as jnp
from jax import lax
from jax.experimental import pallas as pl
from jax.experimental.pallas import tpu as pltpu
from jax.sharding import PartitionSpec as P

HEADS = 8
F32 = jnp.float32
BF16 = jnp.bfloat16


def layer_norm(values):
    wide = values.astype(F32)
    center = wide - jnp.mean(wide, axis=-1, keepdims=True)
    spread = jnp.mean(center * center, axis=-1, keepdims=True)
    return (center * lax.rsqrt(spread + 1e-05)).astype(BF16)


def project(values, matrix):
    return jnp.dot(values, matrix, preferred_element_type=F32)


def product(left, right, left_dim, right_dim):
    dims = (((left_dim,), (right_dim,)), ((), ()))
    return lax.dot_general(left, right, dims, preferred_element_type=F32)


def head_masks(feature, kind):
    size = feature // HEADS
    lanes = lax.broadcasted_iota(jnp.int32, (1, feature), 1)
    return [
        jnp.where((lanes >= head * size) & (lanes < (head + 1) * size), 1.0, 0.0).astype(kind)
        for head in range(HEADS)
    ]


def spread_heads(rows, masks):
    return jnp.concatenate([rows * mask for mask in masks], axis=0)


def time_step(tokens, first_frame, end_frame, attn_ref, in_ref, out_ref, ones_ref):
    tracks, frames, feature = tokens.shape
    scale = 1.0 / math.sqrt(feature // HEADS)
    masks = head_masks(feature, BF16)
    wide = tokens.reshape(tracks * frames, feature).astype(F32)
    normed = layer_norm(wide)
    queries = project(normed, attn_ref[0]).astype(BF16)
    keys = project(normed, attn_ref[1]).astype(BF16)
    values = project(normed, attn_ref[2]).astype(BF16)
    lane = lax.broadcasted_iota(jnp.int32, (1, frames), 1)
    row = lax.broadcasted_iota(jnp.int32, (frames, feature), 0)
    mixed, vis = [], []
    for track in range(tracks):
        part = slice(track * frames, (track + 1) * frames)
        seen = (lane >= first_frame[track]) & (lane < end_frame[track])
        scores = product(queries[part], spread_heads(keys[part], masks), 1, 1)
        weights = []
        for head in range(HEADS):
            own = scores[:, head * frames : (head + 1) * frames] * scale
            own = jnp.where(seen, own, -1e30)
            top = jnp.max(own, axis=-1, keepdims=True)
            weights.append(jnp.exp(own - top).astype(BF16))
        weights = jnp.concatenate(weights, axis=1)
        summed = project(weights, spread_heads(values[part], masks))
        total = project(weights, ones_ref[...])
        mixed.append((summed / total).astype(BF16))
        shown = (row >= first_frame[track]) & (row < end_frame[track])
        vis.append(jnp.where(shown, 1.0, 0.0).astype(F32))
    mixed = jnp.concatenate(mixed, axis=0)
    vis = jnp.concatenate(vis, axis=0)
    first = wide + vis * project(mixed, attn_ref[3])
    hidden = jax.nn.gelu(project(layer_norm(first), in_ref[...]), approximate=True).astype(BF16)
    return first + vis * project(hidden, out_ref[...])


def fill_ones(ones_ref, feature):
    rows = ones_ref.shape[0] // HEADS
    for head, mask in enumerate(head_masks(feature, F32)):
        ones_ref[head * rows : (head + 1) * rows, :] = jnp.broadcast_to(mask, (rows, feature)).astype(BF16)


def few_queries(spread_queries, keys, values, masks):
    feature = keys.shape[1]
    scores = product(spread_queries, keys, 1, 1) * (1.0 / math.sqrt(feature // HEADS))
    top = jnp.max(scores, axis=-1, keepdims=True)
    weights = jnp.exp(scores - top)
    total = jnp.sum(weights, axis=-1, keepdims=True)
    summed = project(weights.astype(BF16), values) / total
    count = spread_queries.shape[0] // HEADS
    mixed = summed[:count] * masks[0]
    for head in range(1, HEADS):
        mixed = mixed + summed[head * count : (head + 1) * count] * masks[head]
    return mixed.astype(BF16)


def frame_step(wide, key_c, value_c, query_b, attn_ref, virtual_ref, query_ref, ones_ref):
    frames, tracks, feature = wide.shape
    n_virtual = virtual_ref.shape[0]
    scale = 1.0 / math.sqrt(feature // HEADS)
    masks = head_masks(feature, BF16)
    wide_masks = head_masks(feature, F32)
    wide = wide.reshape(frames * tracks, feature).astype(F32)
    virtual_part = [slice(f * n_virtual, (f + 1) * n_virtual) for f in range(frames)]
    cross = [few_queries(query_ref[...], key_c[f], value_c[f], wide_masks) for f in range(frames)]
    base = jnp.concatenate([virtual_ref[...].astype(F32)] * frames, axis=0)
    first = base + project(jnp.concatenate(cross, axis=0), attn_ref[0, 3])
    normed_w = layer_norm(first)
    query_s = project(normed_w, attn_ref[1, 0]).astype(BF16)
    key_s = project(normed_w, attn_ref[1, 1]).astype(BF16)
    value_s = project(normed_w, attn_ref[1, 2]).astype(BF16)
    among = [
        few_queries(spread_heads(query_s[part], masks), key_s[part], value_s[part], wide_masks)
        for part in virtual_part
    ]
    second = first + project(jnp.concatenate(among, axis=0), attn_ref[1, 3])
    normed_b = layer_norm(second)
    key_b = project(normed_b, attn_ref[2, 1]).astype(BF16)
    value_b = project(normed_b, attn_ref[2, 2]).astype(BF16)
    back = []
    for frame in range(frames):
        part = virtual_part[frame]
        scores = product(spread_heads(key_b[part], masks), query_b[frame], 1, 1) * scale
        scores = scores.reshape(HEADS, n_virtual, tracks)
        top = jnp.max(scores, axis=1, keepdims=True)
        weights = jnp.exp(scores - top).astype(BF16).reshape(HEADS * n_virtual, tracks)
        summed = product(weights, spread_heads(value_b[part], masks), 0, 0)
        total = product(weights, ones_ref[...], 0, 0)
        back.append((summed / total).astype(BF16))
    return wide + project(jnp.concatenate(back, axis=0), attn_ref[2, 3])


class Exchange:
    def __init__(self, shape):
        self.n_sub = shape["sub"]
        self.count = shape["track"] * shape["sub"]
        self.me = lax.axis_index("track") * self.n_sub + lax.axis_index("sub")
        self.offsets = sorted(range(1, self.count), key=lambda j: abs(2 * j - self.count))

    def device(self, peer):
        return {"track": peer // self.n_sub, "sub": peer % self.n_sub}

    def greet(self):
        barrier = pltpu.get_barrier_semaphore()
        for offset in self.offsets:
            pl.semaphore_signal(
                barrier,
                inc=1,
                device_id=self.device(lax.rem(self.me + offset, self.count)),
                device_id_type=pl.DeviceIdType.MESH,
            )

    def admit(self):
        pl.semaphore_wait(pltpu.get_barrier_semaphore(), self.count - 1)

    def send(self, source_of, target, send_sem, recv_sem, local_sem):
        for offset in self.offsets:
            peer = lax.rem(self.me + offset, self.count)
            pltpu.make_async_remote_copy(
                src_ref=source_of(peer),
                dst_ref=target,
                send_sem=send_sem,
                recv_sem=recv_sem,
                device_id=self.device(peer),
                device_id_type=pl.DeviceIdType.MESH,
            ).start()
        pltpu.make_async_copy(source_of(self.me), target, local_sem).start()


def await_bytes(ref, sem):
    pltpu.make_async_copy(ref, ref, sem).wait()


def layer_kernel(
    shape, n_time, frame_group,
    vis_ref, tok_ref, attn_ref, in_ref, out_ref, virt_hbm, virtual_ref, dest_ref,
    time_ones, frame_ones, sort_ref, home_ref, query_ref, virt_ref,
    slab, inbox, x_ref, key_ref, value_ref, qb_ref, outbox,
    weight_sem, send1, recv1, local1, send2, recv2, local2,
):
    step = pl.program_id(0)
    group, frames, feature = tok_ref.shape
    exchange = Exchange(shape)
    count = exchange.count
    each = frames // count
    chunk = count * group
    tracks = chunk * n_time
    own_tracks = n_time * group
    lag = n_time // 2
    frame_at = n_time + lag

    @pl.when(step == 0)
    def _():
        exchange.greet()
        pltpu.make_async_copy(virt_hbm, virt_ref, weight_sem).start()
        fill_ones(time_ones, feature)

    @pl.when(step < n_time)
    def _():
        begin = [vis_ref[0, step * group + i] for i in range(group)]
        end = [vis_ref[1, step * group + i] for i in range(group)]
        after = time_step(tok_ref[...], begin, end, attn_ref, in_ref, out_ref, time_ones)
        for i in range(group):
            block = after[i * frames : (i + 1) * frames].reshape(count, each, feature)
            slab[step, :, i] = block.astype(BF16)

        @pl.when(step == 0)
        def _():
            exchange.admit()

        exchange.send(
            lambda peer: slab.at[step, peer], inbox.at[step, exchange.me], send1, recv1.at[step], local1.at[step]
        )

    @pl.when(step == lag)
    def _():
        pltpu.make_async_copy(virt_hbm, virt_ref, weight_sem).wait()
        fill_ones(frame_ones, feature)
        query = project(layer_norm(virtual_ref[...]), virt_ref[0, 0]).astype(BF16)
        query_ref[...] = spread_heads(query, head_masks(feature, BF16))
        row = lax.broadcasted_iota(jnp.int32, (chunk * each, chunk * each), 0)
        col = lax.broadcasted_iota(jnp.int32, (chunk * each, chunk * each), 1)
        sort_ref[...] = jnp.where(col == row % chunk * each + row // chunk, 1.0, 0.0).astype(BF16)
        row = lax.broadcasted_iota(jnp.int32, (tracks, tracks), 0)
        col = lax.broadcasted_iota(jnp.int32, (tracks, tracks), 1)
        track = row % own_tracks
        place = track // group * chunk + row // own_tracks * group + track % group
        home_ref[...] = jnp.where(col == place, 1.0, 0.0).astype(BF16)

    def arrive(index):
        await_bytes(inbox.at[index, pl.ds(0, count - 1)], recv1.at[index])
        await_bytes(inbox.at[index, 0], local1.at[index])
        rows = inbox[index].reshape(chunk * each, feature)
        rows = project(sort_ref[...], rows).astype(BF16)
        normed = layer_norm(rows)
        place = pl.ds(pl.multiple_of(index * chunk, chunk), chunk)
        for ref, values in (
            (x_ref, rows),
            (key_ref, project(normed, virt_ref[0, 1]).astype(BF16)),
            (value_ref, project(normed, virt_ref[0, 2]).astype(BF16)),
            (qb_ref, project(normed, virt_ref[2, 0]).astype(BF16)),
        ):
            ref[:, place] = values.reshape(each, chunk, feature)

    @pl.when((step >= lag) & (step < frame_at))
    def _():
        arrive(step - lag)

    @pl.when(step >= frame_at)
    def _():
        first = (step - frame_at) * frame_group
        part = pl.ds(first, frame_group)
        after = frame_step(
            x_ref[part], key_ref[part], value_ref[part], qb_ref[part], virt_ref, virtual_ref, query_ref, frame_ones
        ).astype(BF16)
        for f in range(frame_group):
            block = project(home_ref[...], after[f * tracks : (f + 1) * tracks]).astype(BF16)
            outbox[:, first + f] = block.reshape(count, own_tracks, feature)
        exchange.send(
            lambda peer: outbox.at[peer, part],
            dest_ref.at[pl.ds(exchange.me * each + first, frame_group)],
            send2,
            recv2,
            local2,
        )

    @pl.when(step == pl.num_programs(0) - 1)
    def _():
        await_bytes(slab.at[:, pl.ds(0, count - 1)], send1)
        others = dest_ref.at[pl.ds(0, (count - 1) * each)]
        await_bytes(dest_ref.at[pl.ds(0, each)], local2)
        await_bytes(others, send2)
        await_bytes(others, recv2)


WHOLE = pl.BlockSpec(memory_space=pltpu.VMEM)
ANY = pl.BlockSpec(memory_space=pl.ANY)
LIMIT = 60 * 1024 * 1024


def shards(shape, tokens, visible, time_attn, mlp_in, mlp_out, virt_attn, virtual):
    own_tracks, frames, feature = tokens.shape
    n_virtual = virtual.shape[0]
    count = shape["track"] * shape["sub"]
    group, frame_group = 2, 2
    each = frames // count
    n_time = own_tracks // group
    tracks = count * own_tracks
    chunk = count * group
    by_frame = pltpu.VMEM((each, tracks, feature), BF16)
    dma = pltpu.SemaphoreType.DMA
    result = pl.pallas_call(
        functools.partial(layer_kernel, shape, n_time, frame_group),
        grid=(n_time + n_time // 2 + each // frame_group,),
        in_specs=[
            pl.BlockSpec(memory_space=pltpu.SMEM),
            pl.BlockSpec((group, frames, feature), lambda i: (jnp.minimum(i, n_time - 1), 0, 0)),
            WHOLE, WHOLE, WHOLE, ANY, WHOLE,
        ],
        out_specs=ANY,
        out_shape=jax.ShapeDtypeStruct((frames, own_tracks, feature), BF16),
        scratch_shapes=[
            pltpu.VMEM((HEADS * frames, feature), BF16),
            pltpu.VMEM((HEADS * n_virtual, feature), BF16),
            pltpu.VMEM((chunk * each, chunk * each), BF16),
            pltpu.VMEM((tracks, tracks), BF16),
            pltpu.VMEM((HEADS * n_virtual, feature), BF16),
            pltpu.VMEM(virt_attn.shape, BF16),
            pltpu.VMEM((n_time, count, group, each, feature), BF16),
            pltpu.VMEM((n_time, count, group, each, feature), BF16),
            by_frame, by_frame, by_frame, by_frame,
            pltpu.VMEM((count, each, own_tracks, feature), BF16),
            dma, dma, dma((n_time,)), dma((n_time,)), dma, dma, dma,
        ],
        compiler_params=pltpu.CompilerParams(vmem_limit_bytes=LIMIT, collective_id=0, has_side_effects=True),
    )(visible.T, tokens, time_attn, mlp_in, mlp_out, virt_attn, virtual)
    return jnp.swapaxes(result, 0, 1)


def solution(mesh):
    placed = (
        P(("groups", "track", "sub"), None, None),
        P(("groups", "track", "sub"), None),
        P(),
        P(),
        P(),
        P(),
        P(),
    )
    return jax.shard_map(
        functools.partial(shards, dict(mesh.shape)),
        mesh=mesh,
        in_specs=placed,
        out_specs=P(("groups", "track", "sub"), None, None),
        check_vma=False,
    )
```
